32 devices in a mesh: group: 2 (over y), frame: 4 (over z), space: 2 (over x), head: 2 (over core).
Axes of the slice: x: 2, y: 2, z: 4, core: 2. Of those that a mesh axis runs over, the one named last changes fastest.
Arguments:
- queries: bfloat16 [8, 8, 48, 3072], P(('group', 'frame'), 'space', None, 'head'), parts along dimension 0, may hold values from -8 to 8
- keys: bfloat16 [8, 8, 48, 3072], P(('group', 'frame'), 'space', None, 'head'), parts along dimension 0, may hold values from -8 to 8
- values: bfloat16 [8, 8, 48, 3072], P(('group', 'frame'), 'space', None, 'head'), parts along dimension 0, may hold values from -6 to 6
- flags: int32 [4, 4], replicated, may hold values from 0 to 1, as said below
- widths: int32 [4], replicated, may hold values from 0 to 8, as said below
Outputs:
- attended: bfloat16 [8, 8, 48, 3072], P(('group', 'frame'), 'space', None, 'head'), parts along dimension 0
The draws below stay inside these ranges and needn't reach their ends.
There are 2 independent parts, one for each index of `group`. The reference program is written for one: setup_inputs(seed, part) draws one part's arguments, and reference() takes and returns one part's arrays. A program takes and returns all parts, laid end to end along the dimension named above; an argument that names none is the same for every part. Nothing has to cross between parts.
Inputs may be any that keep to these rules, and one draw needn't show every extreme that they name: flags[f, g] = 1 wherever |f - g| <= 1, and flags[0, 3] = flags[3, 0] = 0. widths[0] = 8, and widths never rise with the frame distance.
All inputs are finite; a program needn't handle non-finite values.
Results may differ from the reference program's by a relative error of at most 0.006.
Values may be sent and summed in bfloat16 or wider, within the bound.
A program may use at most 128 MiB of HBM per device.

```python
import jax
import jax.numpy as jnp
from jax import lax

HEADS = 24
HEAD_DIM = 128
PC = 48
FRAMES = 4
ROWS = 8


def draw_queries(key, part):
    shape = (FRAMES, ROWS, PC, HEADS, HEAD_DIM)
    base = jax.random.normal(jax.random.fold_in(key, 11), shape, jnp.float32)
    result = jnp.clip(1.5 * base, -8.0, 8.0)
    return result.reshape(FRAMES, ROWS, PC, HEADS * HEAD_DIM).astype(jnp.bfloat16)


def draw_keys(key, part):
    shape = (FRAMES, ROWS, PC, HEADS, HEAD_DIM)
    base = jax.random.normal(jax.random.fold_in(key, 21), shape, jnp.float32)
    result = jnp.clip(base, -6.0, 6.0)
    return result.reshape(FRAMES, ROWS, PC, HEADS * HEAD_DIM).astype(jnp.bfloat16)


def draw_flags(key, part):
    levels = jax.random.randint(jax.random.fold_in(key, 31), (FRAMES, FRAMES), 0, 16)
    frame_ids = jnp.arange(FRAMES, dtype=jnp.int32)
    distance = jnp.abs(frame_ids[:, None] - frame_ids[None, :])
    base_flags = (levels * distance < 24).astype(jnp.int32)
    return jnp.where(distance == FRAMES - 1, 0, base_flags).astype(jnp.int32)


def draw_widths(key, part):
    distance = jnp.arange(FRAMES, dtype=jnp.int32)
    first_band = jax.random.randint(jax.random.fold_in(key, 41), (), 1, 3)
    band_count = jnp.zeros((FRAMES,), jnp.int32)
    for level in range(8):
        band_count = band_count + (distance >= first_band * 2 ** level).astype(jnp.int32)
    extra_drop = jax.random.randint(jax.random.fold_in(key, 42), (FRAMES,), 0, 2)
    extra_drop = jnp.where(distance == 0, 0, extra_drop)
    shifts = jnp.minimum(band_count + extra_drop, 30)
    raw_widths = jnp.right_shift(jnp.full((FRAMES,), ROWS, jnp.int32), shifts)
    return lax.cummin(raw_widths, axis=0).astype(jnp.int32)


def block_scale(stream_key, extent, pieces, least, largest):
    def one(dim, parts):
        heights = jax.random.uniform(jax.random.fold_in(jax.random.fold_in(stream_key, 6), dim), (parts,), jnp.float32, least / len(pieces), largest / len(pieces))
        return jnp.repeat(jnp.exp(heights), extent[dim] // parts).reshape((-1,) + (1,) * (len(extent) - dim - 1))

    factor_of = one(*pieces[0])
    for cut in pieces[1:]:
        factor_of = factor_of * one(*cut)
    return factor_of


def bell_draw(stream_key, dims, spread, reach, split=(), kind=jnp.bfloat16):
    values = jax.random.normal(stream_key, dims, jnp.float32) * spread
    if len(split) > 0:
        values = block_scale(stream_key, dims, split, -0.22, 0.18) * values
    return jnp.clip(values, min=-reach, max=reach).astype(kind)


def setup_inputs(seed: int = 0, part: int = 0) -> dict:
    arg_keys = jax.random.split(jax.random.key(seed), 6)
    part_keys = jax.random.split(jax.random.fold_in(arg_keys[5], part), 6)
    return {
        "queries": draw_queries(jax.random.fold_in(jax.random.fold_in(arg_keys[5], part), 71), part),
        "keys": draw_keys(jax.random.fold_in(jax.random.fold_in(arg_keys[5], part), 71), part),
        "values": bell_draw(part_keys[2], (FRAMES, ROWS, PC, HEADS * HEAD_DIM), 1.0, 6.0, ((0, 4), (1, 2), (3, 2))),
        "flags": draw_flags(jax.random.fold_in(arg_keys[5], 71), part),
        "widths": draw_widths(jax.random.fold_in(arg_keys[5], 71), part),
    }


def reference(queries, keys, values, flags, widths):
    frame_count, row_count, column_count, features = queries.shape
    head_count = features // HEAD_DIM
    per_frame = row_count * column_count
    scale = 1.0 / (HEAD_DIM ** 0.5)
    query_tok = queries.reshape(frame_count, per_frame, head_count, HEAD_DIM)
    key_tok = keys.reshape(frame_count * per_frame, head_count, HEAD_DIM)
    value_tok = values.reshape(frame_count * per_frame, head_count, HEAD_DIM)
    token_ids = jnp.arange(frame_count * per_frame, dtype=jnp.int32)
    key_frame = token_ids // per_frame
    key_row = (token_ids // column_count) % row_count
    query_row = jnp.arange(per_frame, dtype=jnp.int32) // column_count

    def frame_out(query_frame):
        frame_query = lax.dynamic_index_in_dim(query_tok, query_frame, 0, False)
        flag_row = lax.dynamic_index_in_dim(flags, query_frame, 0, False)
        reach_rows = widths[jnp.abs(query_frame - key_frame)]
        allowed = (flag_row[key_frame] > 0)[None, :] & (
            jnp.abs(query_row[:, None] - key_row[None, :]) <= reach_rows[None, :])

        def head_out(head):
            head_query = lax.dynamic_index_in_dim(frame_query, head, 1, False)
            head_key = lax.dynamic_index_in_dim(key_tok, head, 1, False)
            head_value = lax.dynamic_index_in_dim(value_tok, head, 1, False)
            scores = jnp.dot(head_query, head_key.T, preferred_element_type=jnp.float32) * scale
            scores = jnp.where(allowed, scores, -jnp.inf)
            top = jnp.max(scores, axis=1, keepdims=True)
            weights = jnp.where(allowed, jnp.exp(scores - top), 0.0)
            total = jnp.sum(weights, axis=1, keepdims=True)
            blended = jnp.dot(weights.astype(jnp.bfloat16), head_value, preferred_element_type=jnp.float32)
            return blended / total

        outputs = lax.map(head_out, jnp.arange(head_count, dtype=jnp.int32))
        return jnp.transpose(outputs, (1, 0, 2)).reshape(per_frame, features)

    result = lax.map(frame_out, jnp.arange(frame_count, dtype=jnp.int32))
    return result.reshape(queries.shape).astype(jnp.bfloat16)
```

```python
import functools
import math

import jax
import jax.numpy as jnp
from jax import lax
from jax.experimental import pallas as pl
from jax.experimental.pallas import tpu as pltpu
from jax.sharding import PartitionSpec as P

HEAD_DIM = 128
NEG_FILL = -1e30
SCALE = math.log2(math.e) / HEAD_DIM**0.5
MESH = pl.DeviceIdType.MESH


def kernel(
    frames,
    parts,
    heads,
    q_ref,
    k_ref,
    v_ref,
    flags_ref,
    widths_ref,
    row_ref,
    col_ref,
    out_ref,
    kv,
    qb,
    ob,
    dist,
    top,
    total,
    acc,
    local_sem,
    xkv_send,
    xkv_recv,
    xq_send,
    xq_recv,
    z_send,
    z_recv,
    o_local,
    o_send,
    o_recv,
):
    frame = lax.axis_index("frame")
    part = lax.axis_index("space")
    rows = q_ref.shape[0]
    tokens = parts * rows
    tile = 128 if tokens % 128 == 0 else rows
    far = frames - 2
    LEFT, RIGHT = 0, 1

    def lanes(ref, head):
        return ref.at[:, pl.ds(pl.multiple_of(head * HEAD_DIM, HEAD_DIM), HEAD_DIM)]

    def peer(j):
        return lax.rem(part + j, parts)

    barrier = pltpu.get_barrier_semaphore()
    for j in range(1, parts):
        pl.semaphore_signal(barrier, inc=1, device_id={"space": peer(j)}, device_id_type=MESH)

    @pl.when(frame > 0)
    def _():
        pl.semaphore_signal(barrier, inc=1, device_id={"frame": frame - 1}, device_id_type=MESH)

    @pl.when(frame < frames - 1)
    def _():
        pl.semaphore_signal(barrier, inc=1, device_id={"frame": frame + 1}, device_id_type=MESH)

    def local_copies(h):
        mine = part * heads + h
        return (
            pltpu.make_async_copy(lanes(k_ref, mine), kv.at[frame, h, part, 0], local_sem.at[0, h]),
            pltpu.make_async_copy(lanes(v_ref, mine), kv.at[frame, h, part, 1], local_sem.at[1, h]),
            pltpu.make_async_copy(lanes(q_ref, mine), qb.at[h, part], local_sem.at[2, h]),
        )

    def kv_exchange(h, j, i, src_ref):
        return pltpu.make_async_remote_copy(
            src_ref=lanes(src_ref, peer(j) * heads + h),
            dst_ref=kv.at[frame, h, part, i],
            send_sem=xkv_send.at[i, j - 1, h],
            recv_sem=xkv_recv.at[i, j - 1, h],
            device_id={"space": peer(j)},
            device_id_type=MESH,
        )

    def q_exchange(h, j):
        return pltpu.make_async_remote_copy(
            src_ref=lanes(q_ref, peer(j) * heads + h),
            dst_ref=qb.at[h, part],
            send_sem=xq_send.at[j - 1, h],
            recv_sem=xq_recv.at[j - 1, h],
            device_id={"space": peer(j)},
            device_id_type=MESH,
        )

    def o_exchange(h, j):
        return pltpu.make_async_remote_copy(
            src_ref=ob.at[h, pl.ds(pl.multiple_of(peer(j) * rows, rows), rows)],
            dst_ref=lanes(out_ref, part * heads + h),
            send_sem=o_send.at[j - 1, h],
            recv_sem=o_recv.at[j - 1, h],
            device_id={"space": peer(j)},
            device_id_type=MESH,
        )

    def o_keep(h):
        return pltpu.make_async_copy(
            ob.at[h, pl.ds(pl.multiple_of(part * rows, rows), rows)],
            lanes(out_ref, part * heads + h),
            o_local.at[h],
        )

    def hop(side, step, h, p, i, src=None):
        towards = 1 if side == RIGHT else -1
        owner = frame - towards * (step - 1)
        return pltpu.make_async_remote_copy(
            src_ref=kv.at[owner, h, p, i] if src is None else src,
            dst_ref=kv.at[owner, h, p, i],
            send_sem=z_send.at[side, step - 1, h, p, i],
            recv_sem=z_recv.at[side, step - 1, h, p, i],
            device_id={"frame": frame + towards},
            device_id_type=MESH,
        )

    def can_send(side, step):
        if side == RIGHT:
            return (frame < frames - 1) & (frame - (step - 1) >= 0)
        return (frame > 0) & (frame + (step - 1) <= frames - 1)

    def gets(side, step):
        if side == RIGHT:
            return frame - step >= 0
        return frame + step <= frames - 1

    def landed(side, step, h, p, i):
        towards = 1 if side == RIGHT else -1
        owner = frame - towards * step
        return pltpu.make_async_remote_copy(
            src_ref=kv.at[owner, h, p, i],
            dst_ref=kv.at[owner, h, p, i],
            send_sem=z_send.at[side, step - 1, h, p, i],
            recv_sem=z_recv.at[side, step - 1, h, p, i],
            device_id={"frame": frame - towards},
            device_id_type=MESH,
        )

    def each_head(body):
        @pl.loop(0, heads)
        def _(h):
            body(h)

    pl.semaphore_wait(
        barrier,
        parts - 1 + jnp.where(frame > 0, 1, 0) + jnp.where(frame < frames - 1, 1, 0),
    )

    def open_head(h):
        mine = part * heads + h
        for j in range(1, parts):
            kv_exchange(h, j, 0, k_ref).start()
            kv_exchange(h, j, 1, v_ref).start()
        for side in (LEFT, RIGHT):

            @pl.when(can_send(side, 1))
            def _():
                hop(side, 1, h, part, 0, lanes(k_ref, mine)).start()
                hop(side, 1, h, part, 1, lanes(v_ref, mine)).start()

    each_head(open_head)

    def open_queries(h):
        for copy in local_copies(h):
            copy.start()
        for j in range(1, parts):
            q_exchange(h, j).start()

    each_head(open_queries)

    dist[...] = jnp.abs(row_ref[...] - col_ref[...])
    top[...] = jnp.full(top.shape, NEG_FILL, jnp.float32)
    total[...] = jnp.zeros(total.shape, jnp.float32)
    acc[...] = jnp.zeros(acc.shape, jnp.float32)

    def pass_parts(h):
        for j in range(1, parts):
            p = lax.rem(part - j + parts, parts)
            for i in (0, 1):
                kv_exchange(h, j, i, (k_ref, v_ref)[i]).wait_recv()
            for side in (LEFT, RIGHT):

                @pl.when(can_send(side, 1))
                def _():
                    for i in (0, 1):
                        hop(side, 1, h, p, i).start()

    each_head(pass_parts)

    def update(h, g):
        gap = jnp.abs(frame - g)
        reach = jnp.where(flags_ref[frame, g] > 0, widths_ref[gap], -1)
        keys = kv[g, h, :, 0].reshape(tokens, HEAD_DIM)
        vals = kv[g, h, :, 1].reshape(tokens, HEAD_DIM)
        queries = qb[h].reshape(tokens, HEAD_DIM)
        for at in range(0, tokens, tile):
            cut = pl.ds(at, tile)
            scores = lax.dot_general(
                queries[at : at + tile],
                keys,
                (((1,), (1,)), ((), ())),
                preferred_element_type=jnp.float32,
            )
            scores = jnp.where(dist[cut, :] <= reach, scores, NEG_FILL)
            old_top = top[h, cut]
            new_top = jnp.maximum(old_top, jnp.max(scores, axis=1, keepdims=True))
            weights = jnp.exp2((scores - new_top) * SCALE)
            keep = jnp.exp2((old_top - new_top) * SCALE)
            top[h, cut] = new_top
            total[h, cut] = total[h, cut] * keep + jnp.sum(weights, axis=1, keepdims=True)
            acc[h, cut] = acc[h, cut] * keep + jnp.dot(
                weights.astype(jnp.bfloat16), vals, preferred_element_type=jnp.float32
            )

    def arrive(step, h):
        for side in (LEFT, RIGHT):

            @pl.when(gets(side, step))
            def _():
                for p in range(parts):
                    for i in (0, 1):
                        landed(side, step, h, p, i).wait_recv()

            if step < far:

                @pl.when(gets(side, step) & can_send(side, step + 1))
                def _():
                    for p in range(parts):
                        for i in (0, 1):
                            hop(side, step + 1, h, p, i).start()

    def blend(step, h):
        @pl.when(frame - step >= 0)
        def _():
            update(h, frame - step)

        @pl.when(frame + step <= frames - 1)
        def _():
            update(h, frame + step)

    for step in range(1, far + 1):

        def advance(h, step=step):
            arrive(step, h)
            if step == 1:
                for copy in local_copies(h):
                    copy.wait()
                for j in range(1, parts):
                    q_exchange(h, j).wait_recv()
                update(h, frame)
            blend(step, h)
            if step == far:
                ob[h] = (acc[h] / total[h]).astype(jnp.bfloat16)
                for j in range(1, parts):
                    o_exchange(h, j).start()
                o_keep(h).start()

        each_head(advance)

    def close_head(h):
        mine = part * heads + h
        o_keep(h).wait()
        for j in range(1, parts):
            o_exchange(h, j).wait()
            q_exchange(h, j).wait_send()
            kv_exchange(h, j, 0, k_ref).wait_send()
            kv_exchange(h, j, 1, v_ref).wait_send()
        for step in range(1, far + 1):
            for side in (LEFT, RIGHT):

                @pl.when(can_send(side, step))
                def _():
                    for p in range(parts):
                        for i in (0, 1):
                            hop(side, step, h, p, i).wait_send()

    each_head(close_head)


def shards(frames, parts, queries, keys, values, flags, widths):
    shape = queries.shape
    columns, features = shape[2], shape[3]
    rows = shape[1] * columns
    heads = features // HEAD_DIM // parts
    tokens = rows * parts
    far = frames - 2
    token_rows = jnp.arange(tokens, dtype=jnp.int32) // columns
    flat = [a.reshape(rows, features) for a in (queries, keys, values)]
    any_spec = pl.BlockSpec(memory_space=pl.ANY)
    vmem = pl.BlockSpec(memory_space=pltpu.VMEM)
    smem = pl.BlockSpec(memory_space=pltpu.SMEM)
    others = max(parts - 1, 1)
    dma = pltpu.SemaphoreType.DMA
    out = pl.pallas_call(
        functools.partial(kernel, frames, parts, heads),
        out_shape=jax.ShapeDtypeStruct((rows, features), jnp.bfloat16),
        in_specs=[any_spec, any_spec, any_spec, smem, smem, vmem, vmem],
        out_specs=any_spec,
        scratch_shapes=[
            pltpu.VMEM((frames, heads, parts, 2, rows, HEAD_DIM), jnp.bfloat16),
            pltpu.VMEM((heads, parts, rows, HEAD_DIM), jnp.bfloat16),
            pltpu.VMEM((heads, tokens, HEAD_DIM), jnp.bfloat16),
            pltpu.VMEM((tokens, tokens), jnp.int32),
            pltpu.VMEM((heads, tokens, 1), jnp.float32),
            pltpu.VMEM((heads, tokens, 1), jnp.float32),
            pltpu.VMEM((heads, tokens, HEAD_DIM), jnp.float32),
            dma((3, heads)),
            dma((2, others, heads)),
            dma((2, others, heads)),
            dma((others, heads)),
            dma((others, heads)),
            dma((2, far, heads, parts, 2)),
            dma((2, far, heads, parts, 2)),
            dma((heads,)),
            dma((others, heads)),
            dma((others, heads)),
        ],
        compiler_params=pltpu.CompilerParams(collective_id=0, has_side_effects=True),
    )(*flat, flags, widths, token_rows[:, None], token_rows[None, :])
    return out.reshape(shape)


def solution(mesh):
    spec = P(("group", "frame"), "space", None, "head")
    return jax.shard_map(
        functools.partial(shards, mesh.shape["frame"], mesh.shape["space"]),
        mesh=mesh,
        in_specs=(spec, spec, spec, P(), P()),
        out_specs=spec,
        check_vma=False,
    )
```

```python
import functools
import math

import jax
import jax.numpy as jnp
from jax import lax
from jax.experimental import pallas as pl
from jax.experimental.pallas import tpu as pltpu
from jax.sharding import PartitionSpec as P

HEAD_DIM = 128
NEG_FILL = -1e30
SCALE = math.log2(math.e) / HEAD_DIM**0.5
MESH = pl.DeviceIdType.MESH


def kernel(
    frames,
    parts,
    heads,
    columns,
    q_ref,
    k_ref,
    v_ref,
    flags_ref,
    widths_ref,
    out_ref,
    kv,
    qb,
    ob,
    dist,
    wb,
    top,
    total,
    acc,
    local_sem,
    xkv_send,
    xkv_recv,
    xq_send,
    xq_recv,
    z_send,
    z_recv,
    o_local,
    o_send,
    o_recv,
):
    frame = lax.axis_index("frame")
    part = lax.axis_index("space")
    rows = q_ref.shape[0]
    tokens = parts * rows
    tile = rows
    far = frames - 2
    LEFT, RIGHT = 0, 1

    def lanes(ref, head):
        return ref.at[:, pl.ds(pl.multiple_of(head * HEAD_DIM, HEAD_DIM), HEAD_DIM)]

    def peer(j):
        return lax.rem(part + j, parts)

    barrier = pltpu.get_barrier_semaphore()
    for j in range(1, parts):
        pl.semaphore_signal(barrier, inc=1, device_id={"space": peer(j)}, device_id_type=MESH)

    @pl.when(frame > 0)
    def _():
        pl.semaphore_signal(barrier, inc=1, device_id={"frame": frame - 1}, device_id_type=MESH)

    @pl.when(frame < frames - 1)
    def _():
        pl.semaphore_signal(barrier, inc=1, device_id={"frame": frame + 1}, device_id_type=MESH)

    def local_copies(h):
        mine = part * heads + h
        return (
            pltpu.make_async_copy(lanes(k_ref, mine), kv.at[frame, h, 0, part], local_sem.at[0, h]),
            pltpu.make_async_copy(lanes(v_ref, mine), kv.at[frame, h, 1, part], local_sem.at[1, h]),
            pltpu.make_async_copy(lanes(q_ref, mine), qb.at[h, part], local_sem.at[2, h]),
        )

    def kv_exchange(h, j, i, src_ref):
        return pltpu.make_async_remote_copy(
            src_ref=lanes(src_ref, peer(j) * heads + h),
            dst_ref=kv.at[frame, h, i, part],
            send_sem=xkv_send.at[i, j - 1, h],
            recv_sem=xkv_recv.at[i, j - 1, h],
            device_id={"space": peer(j)},
            device_id_type=MESH,
        )

    def q_exchange(h, j):
        return pltpu.make_async_remote_copy(
            src_ref=lanes(q_ref, peer(j) * heads + h),
            dst_ref=qb.at[h, part],
            send_sem=xq_send.at[j - 1, h],
            recv_sem=xq_recv.at[j - 1, h],
            device_id={"space": peer(j)},
            device_id_type=MESH,
        )

    def o_exchange(h, j):
        return pltpu.make_async_remote_copy(
            src_ref=ob.at[h, pl.ds(pl.multiple_of(peer(j) * rows, rows), rows)],
            dst_ref=lanes(out_ref, part * heads + h),
            send_sem=o_send.at[j - 1, h],
            recv_sem=o_recv.at[j - 1, h],
            device_id={"space": peer(j)},
            device_id_type=MESH,
        )

    def o_keep(h):
        return pltpu.make_async_copy(
            ob.at[h, pl.ds(pl.multiple_of(part * rows, rows), rows)],
            lanes(out_ref, part * heads + h),
            o_local.at[h],
        )

    def hop(side, step, h, p, i, src=None):
        towards = 1 if side == RIGHT else -1
        owner = frame - towards * (step - 1)
        return pltpu.make_async_remote_copy(
            src_ref=kv.at[owner, h, i, p] if src is None else src,
            dst_ref=kv.at[owner, h, i, p],
            send_sem=z_send.at[side, step - 1, h, p, i],
            recv_sem=z_recv.at[side, step - 1, h, p, i],
            device_id={"frame": frame + towards},
            device_id_type=MESH,
        )

    def can_send(side, step):
        if side == RIGHT:
            return (frame < frames - 1) & (frame - (step - 1) >= 0)
        return (frame > 0) & (frame + (step - 1) <= frames - 1)

    def gets(side, step):
        if side == RIGHT:
            return frame - step >= 0
        return frame + step <= frames - 1

    def landed(side, step, h, p, i):
        towards = 1 if side == RIGHT else -1
        owner = frame - towards * step
        return pltpu.make_async_remote_copy(
            src_ref=kv.at[owner, h, i, p],
            dst_ref=kv.at[owner, h, i, p],
            send_sem=z_send.at[side, step - 1, h, p, i],
            recv_sem=z_recv.at[side, step - 1, h, p, i],
            device_id={"frame": frame - towards},
            device_id_type=MESH,
        )

    def each_head(body):
        @pl.loop(0, heads)
        def _(h):
            body(h)

    pl.semaphore_wait(
        barrier,
        parts - 1 + jnp.where(frame > 0, 1, 0) + jnp.where(frame < frames - 1, 1, 0),
    )

    def open_head(h):
        mine = part * heads + h
        for j in range(1, parts):
            kv_exchange(h, j, 0, k_ref).start()
            kv_exchange(h, j, 1, v_ref).start()
        for side in (LEFT, RIGHT):

            @pl.when(can_send(side, 1))
            def _():
                hop(side, 1, h, part, 0, lanes(k_ref, mine)).start()
                hop(side, 1, h, part, 1, lanes(v_ref, mine)).start()

    each_head(open_head)

    def open_queries(h):
        for copy in local_copies(h):
            copy.start()
        for j in range(1, parts):
            q_exchange(h, j).start()

    each_head(open_queries)

    def row_of(axis):
        at = lax.broadcasted_iota(jnp.int32, (tokens, tokens), axis).astype(jnp.float32)
        return jnp.floor((at + 0.5) * (1.0 / columns))

    dist[...] = jnp.abs(row_of(0) - row_of(1))
    top[...] = jnp.full(top.shape, NEG_FILL, jnp.float32)
    total[...] = jnp.zeros(total.shape, jnp.float32)
    acc[...] = jnp.zeros(acc.shape, jnp.float32)

    def pass_parts(h):
        for j in range(1, parts):
            p = lax.rem(part - j + parts, parts)
            for i in (0, 1):
                kv_exchange(h, j, i, (k_ref, v_ref)[i]).wait_recv()
            for side in (LEFT, RIGHT):

                @pl.when(can_send(side, 1))
                def _():
                    for i in (0, 1):
                        hop(side, 1, h, p, i).start()

    each_head(pass_parts)

    def masked(h, g, at):
        gap = jnp.abs(frame - g)
        reach = jnp.where(flags_ref[frame, g] > 0, widths_ref[gap], -1).astype(jnp.float32)
        cut = pl.ds(at, tile)
        queries = qb[h].reshape(tokens, HEAD_DIM)[at : at + tile]
        keys = kv[g, h, 0].reshape(tokens, HEAD_DIM)
        scores = lax.dot_general(
            queries, keys, (((1,), (1,)), ((), ())), preferred_element_type=jnp.float32
        )
        scores = jnp.where(dist[cut, :] <= reach, scores, NEG_FILL)
        old_top = top[h, cut]
        new_top = jnp.maximum(old_top, jnp.max(scores, axis=1, keepdims=True))
        weights = jnp.exp2((scores - new_top) * SCALE)
        keep = jnp.exp2((old_top - new_top) * SCALE)
        top[h, cut] = new_top
        total[h, cut] = total[h, cut] * keep + jnp.sum(weights, axis=1, keepdims=True)
        return weights.astype(jnp.bfloat16), keep

    def mixed(weights, h, g):
        vals = kv[g, h, 1].reshape(tokens, HEAD_DIM)
        return jnp.dot(weights, vals, preferred_element_type=jnp.float32)

    def update(h, g):
        for at in range(0, tokens, tile):
            cut = pl.ds(at, tile)
            weights, keep = masked(h, g, at)
            acc[h, cut] = acc[h, cut] * keep + mixed(weights, h, g)

    def await_block(side, step, h, i):
        @pl.when(gets(side, step))
        def _():
            for p in range(parts):
                landed(side, step, h, p, i).wait_recv()

    def source(side, step):
        return frame - step if side == RIGHT else frame + step

    def near(step, h, relay):
        for side in (LEFT, RIGHT):
            for i in (0, 1):
                await_block(side, step, h, i)
            if relay:

                @pl.when(gets(side, step) & can_send(side, step + 1))
                def _():
                    for i in (0, 1):
                        for p in range(parts):
                            hop(side, step + 1, h, p, i).start()

    def blend(step, h):
        for side in (LEFT, RIGHT):

            @pl.when(gets(side, step))
            def _():
                update(h, source(side, step))

    def first(h):
        near(1, h, far > 1)
        for copy in local_copies(h):
            copy.wait()
        for j in range(1, parts):
            q_exchange(h, j).wait_recv()
        update(h, frame)
        blend(1, h)

    each_head(first)

    if far > 2:

        @pl.loop(2, far)
        def _(step):
            def middle(h):
                near(step, h, True)
                blend(step, h)

            each_head(middle)

    def last(h):
        for side in (LEFT, RIGHT):
            if far > 1:
                await_block(side, far, h, 0)

                @pl.when(gets(side, far))
                def _():
                    for at in range(0, tokens, tile):
                        weights, keep = masked(h, source(side, far), at)
                        wb[side, pl.ds(at, tile)] = weights
                        acc[h, pl.ds(at, tile)] = acc[h, pl.ds(at, tile)] * keep

        if far > 1:
            for side in (LEFT, RIGHT):
                await_block(side, far, h, 1)

        def finish(p):
            for at in range(0, rows, tile):
                cut = pl.ds(pl.multiple_of(p * rows + at, tile), tile)
                if far > 1:
                    for side in (LEFT, RIGHT):

                        @pl.when(gets(side, far))
                        def _():
                            acc[h, cut] = acc[h, cut] + mixed(
                                wb[side, cut], h, source(side, far)
                            )

                ob[h, cut] = (acc[h, cut] / total[h, cut]).astype(jnp.bfloat16)

        for j in range(1, parts):
            finish(peer(j))
            o_exchange(h, j).start()
        finish(part)
        o_keep(h).start()

    each_head(last)

    def close_head(h):
        o_keep(h).wait()
        for j in range(1, parts):
            o_exchange(h, j).wait()
            q_exchange(h, j).wait_send()
            kv_exchange(h, j, 0, k_ref).wait_send()
            kv_exchange(h, j, 1, v_ref).wait_send()

        @pl.loop(1, far + 1)
        def _(step):
            for side in (LEFT, RIGHT):

                @pl.when(can_send(side, step))
                def _():
                    for p in range(parts):
                        for i in (0, 1):
                            hop(side, step, h, p, i).wait_send()

    each_head(close_head)


def shards(frames, parts, queries, keys, values, flags, widths):
    shape = queries.shape
    columns, features = shape[2], shape[3]
    rows = shape[1] * columns
    heads = features // HEAD_DIM // parts
    tokens = rows * parts
    far = frames - 2
    flat = [a.reshape(rows, features) for a in (queries, keys, values)]
    any_spec = pl.BlockSpec(memory_space=pl.ANY)
    smem = pl.BlockSpec(memory_space=pltpu.SMEM)
    others = max(parts - 1, 1)
    dma = pltpu.SemaphoreType.DMA
    out = pl.pallas_call(
        functools.partial(kernel, frames, parts, heads, columns),
        out_shape=pltpu.VMEM((rows, features), jnp.bfloat16),
        in_specs=[any_spec, any_spec, any_spec, smem, smem],
        out_specs=pl.BlockSpec(memory_space=pltpu.VMEM),
        scratch_shapes=[
            pltpu.VMEM((frames, heads, 2, parts, rows, HEAD_DIM), jnp.bfloat16),
            pltpu.VMEM((heads, parts, rows, HEAD_DIM), jnp.bfloat16),
            pltpu.VMEM((heads, tokens, HEAD_DIM), jnp.bfloat16),
            pltpu.VMEM((tokens, tokens), jnp.float32),
            pltpu.VMEM((2, tokens, tokens), jnp.bfloat16),
            pltpu.VMEM((heads, tokens, 1), jnp.float32),
            pltpu.VMEM((heads, tokens, 1), jnp.float32),
            pltpu.VMEM((heads, tokens, HEAD_DIM), jnp.float32),
            dma((3, heads)),
            dma((2, others, heads)),
            dma((2, others, heads)),
            dma((others, heads)),
            dma((others, heads)),
            dma((2, far, heads, parts, 2)),
            dma((2, far, heads, parts, 2)),
            dma((heads,)),
            dma((others, heads)),
            dma((others, heads)),
        ],
        compiler_params=pltpu.CompilerParams(collective_id=0, has_side_effects=True),
    )(*flat, flags, widths)
    return out.reshape(shape)


def solution(mesh):
    spec = P(("group", "frame"), "space", None, "head")
    return jax.shard_map(
        functools.partial(shards, mesh.shape["frame"], mesh.shape["space"]),
        mesh=mesh,
        in_specs=(spec, spec, spec, P(), P()),
        out_specs=spec,
        check_vma=False,
    )
```

```python
import functools
import math

import jax
import jax.numpy as jnp
from jax import lax
from jax.experimental import pallas as pl
from jax.experimental.pallas import tpu as pltpu
from jax.sharding import PartitionSpec as P

HEAD_DIM = 128
NEG_FILL = -1e30
SCALE = math.log2(math.e) / HEAD_DIM**0.5
MESH = pl.DeviceIdType.MESH


def kernel(
    frames,
    parts,
    heads,
    columns,
    q_ref,
    k_ref,
    v_ref,
    flags_in,
    widths_in,
    out_ref,
    kv,
    qb,
    ob,
    dist,
    wb,
    top,
    total,
    acc,
    local_sem,
    xkv_send,
    xkv_recv,
    xq_send,
    xq_recv,
    z_send,
    z_recv,
    o_local,
    o_send,
    o_recv,
    flags_ref,
    widths_ref,
    table_sem,
):
    frame = lax.axis_index("frame")
    part = lax.axis_index("space")
    rows = q_ref.shape[0]
    tokens = parts * rows
    tile = rows
    far = frames - 2
    LEFT, RIGHT = 0, 1

    def lanes(ref, head):
        return ref.at[:, pl.ds(pl.multiple_of(head * HEAD_DIM, HEAD_DIM), HEAD_DIM)]

    def peer(j):
        return lax.rem(part + j, parts)

    barrier = pltpu.get_barrier_semaphore()
    for j in range(1, parts):
        pl.semaphore_signal(barrier, inc=1, device_id={"space": peer(j)}, device_id_type=MESH)

    @pl.when(frame > 0)
    def _():
        pl.semaphore_signal(barrier, inc=1, device_id={"frame": frame - 1}, device_id_type=MESH)

    @pl.when(frame < frames - 1)
    def _():
        pl.semaphore_signal(barrier, inc=1, device_id={"frame": frame + 1}, device_id_type=MESH)

    def local_copies(h):
        mine = part * heads + h
        return (
            pltpu.make_async_copy(lanes(k_ref, mine), kv.at[frame, h, 0, part], local_sem.at[0, h]),
            pltpu.make_async_copy(lanes(v_ref, mine), kv.at[frame, h, 1, part], local_sem.at[1, h]),
            pltpu.make_async_copy(lanes(q_ref, mine), qb.at[h, part], local_sem.at[2, h]),
        )

    def kv_exchange(h, j, i, src_ref):
        return pltpu.make_async_remote_copy(
            src_ref=lanes(src_ref, peer(j) * heads + h),
            dst_ref=kv.at[frame, h, i, part],
            send_sem=xkv_send.at[i, j - 1, h],
            recv_sem=xkv_recv.at[i, j - 1, h],
            device_id={"space": peer(j)},
            device_id_type=MESH,
        )

    def q_exchange(h, j):
        return pltpu.make_async_remote_copy(
            src_ref=lanes(q_ref, peer(j) * heads + h),
            dst_ref=qb.at[h, part],
            send_sem=xq_send.at[j - 1, h],
            recv_sem=xq_recv.at[j - 1, h],
            device_id={"space": peer(j)},
            device_id_type=MESH,
        )

    def o_exchange(h, j):
        return pltpu.make_async_remote_copy(
            src_ref=ob.at[h, pl.ds(pl.multiple_of(peer(j) * rows, rows), rows)],
            dst_ref=lanes(out_ref, part * heads + h),
            send_sem=o_send.at[j - 1, h],
            recv_sem=o_recv.at[j - 1, h],
            device_id={"space": peer(j)},
            device_id_type=MESH,
        )

    def o_keep(h):
        return pltpu.make_async_copy(
            ob.at[h, pl.ds(pl.multiple_of(part * rows, rows), rows)],
            lanes(out_ref, part * heads + h),
            o_local.at[h],
        )

    def hop(side, step, h, p, i, src=None):
        towards = 1 if side == RIGHT else -1
        owner = frame - towards * (step - 1)
        return pltpu.make_async_remote_copy(
            src_ref=kv.at[owner, h, i, p] if src is None else src,
            dst_ref=kv.at[owner, h, i, p],
            send_sem=z_send.at[side, step - 1, h, p, i],
            recv_sem=z_recv.at[side, step - 1, h, p, i],
            device_id={"frame": frame + towards},
            device_id_type=MESH,
        )

    def can_send(side, step):
        if side == RIGHT:
            return (frame < frames - 1) & (frame - (step - 1) >= 0)
        return (frame > 0) & (frame + (step - 1) <= frames - 1)

    def gets(side, step):
        if side == RIGHT:
            return frame - step >= 0
        return frame + step <= frames - 1

    def landed(side, step, h, p, i):
        towards = 1 if side == RIGHT else -1
        owner = frame - towards * step
        return pltpu.make_async_remote_copy(
            src_ref=kv.at[owner, h, i, p],
            dst_ref=kv.at[owner, h, i, p],
            send_sem=z_send.at[side, step - 1, h, p, i],
            recv_sem=z_recv.at[side, step - 1, h, p, i],
            device_id={"frame": frame - towards},
            device_id_type=MESH,
        )

    def each_head(body):
        @pl.loop(0, heads)
        def _(h):
            body(h)

    pl.semaphore_wait(
        barrier,
        parts - 1 + jnp.where(frame > 0, 1, 0) + jnp.where(frame < frames - 1, 1, 0),
    )

    def open_head(h):
        mine = part * heads + h
        for j in range(1, parts):
            kv_exchange(h, j, 0, k_ref).start()
            kv_exchange(h, j, 1, v_ref).start()
        for side in (LEFT, RIGHT):

            @pl.when(can_send(side, 1))
            def _():
                hop(side, 1, h, part, 0, lanes(k_ref, mine)).start()
                hop(side, 1, h, part, 1, lanes(v_ref, mine)).start()

    each_head(open_head)

    tables = (
        pltpu.make_async_copy(flags_in, flags_ref, table_sem.at[0]),
        pltpu.make_async_copy(widths_in, widths_ref, table_sem.at[1]),
    )
    for copy in tables:
        copy.start()

    def open_queries(h):
        for copy in local_copies(h):
            copy.start()
        for j in range(1, parts):
            q_exchange(h, j).start()

    each_head(open_queries)

    def row_of(axis):
        at = lax.broadcasted_iota(jnp.int32, (tokens, tokens), axis).astype(jnp.float32)
        return jnp.floor((at + 0.5) * (1.0 / columns))

    dist[...] = jnp.abs(row_of(0) - row_of(1))
    top[...] = jnp.full(top.shape, NEG_FILL, jnp.float32)
    total[...] = jnp.zeros(total.shape, jnp.float32)
    acc[...] = jnp.zeros(acc.shape, jnp.float32)

    def pass_parts(h):
        for j in range(1, parts):
            p = lax.rem(part - j + parts, parts)
            for i in (0, 1):
                kv_exchange(h, j, i, (k_ref, v_ref)[i]).wait_recv()
            for side in (LEFT, RIGHT):

                @pl.when(can_send(side, 1))
                def _():
                    for i in (0, 1):
                        hop(side, 1, h, p, i).start()

    each_head(pass_parts)
    for copy in tables:
        copy.wait()

    def masked(h, g, at):
        gap = jnp.abs(frame - g)
        reach = jnp.where(flags_ref[frame, g] > 0, widths_ref[gap], -1).astype(jnp.float32)
        cut = pl.ds(at, tile)
        queries = qb[h].reshape(tokens, HEAD_DIM)[at : at + tile]
        keys = kv[g, h, 0].reshape(tokens, HEAD_DIM)
        scores = lax.dot_general(
            queries, keys, (((1,), (1,)), ((), ())), preferred_element_type=jnp.float32
        )
        scores = jnp.where(dist[cut, :] <= reach, scores, NEG_FILL)
        old_top = top[h, cut]
        new_top = jnp.maximum(old_top, jnp.max(scores, axis=1, keepdims=True))
        weights = jnp.exp2((scores - new_top) * SCALE)
        keep = jnp.exp2((old_top - new_top) * SCALE)
        top[h, cut] = new_top
        total[h, cut] = total[h, cut] * keep + jnp.sum(weights, axis=1, keepdims=True)
        return weights.astype(jnp.bfloat16), keep

    def mixed(weights, h, g):
        vals = kv[g, h, 1].reshape(tokens, HEAD_DIM)
        return jnp.dot(weights, vals, preferred_element_type=jnp.float32)

    def update(h, g):
        for at in range(0, tokens, tile):
            cut = pl.ds(at, tile)
            weights, keep = masked(h, g, at)
            acc[h, cut] = acc[h, cut] * keep + mixed(weights, h, g)

    def await_block(side, step, h, i):
        @pl.when(gets(side, step))
        def _():
            for p in range(parts):
                landed(side, step, h, p, i).wait_recv()

    def source(side, step):
        return frame - step if side == RIGHT else frame + step

    def near(step, h, relay):
        for side in (LEFT, RIGHT):
            for i in (0, 1):
                await_block(side, step, h, i)
            if relay:

                @pl.when(gets(side, step) & can_send(side, step + 1))
                def _():
                    for i in (0, 1):
                        for p in range(parts):
                            hop(side, step + 1, h, p, i).start()

    def blend(step, h):
        for side in (LEFT, RIGHT):

            @pl.when(gets(side, step))
            def _():
                update(h, source(side, step))

    def first(h):
        near(1, h, far > 1)
        for copy in local_copies(h):
            copy.wait()
        for j in range(1, parts):
            q_exchange(h, j).wait_recv()
        update(h, frame)
        blend(1, h)

    each_head(first)

    if far > 2:

        @pl.loop(2, far)
        def _(step):
            def middle(h):
                near(step, h, True)
                blend(step, h)

            each_head(middle)

    def last(h):
        for side in (LEFT, RIGHT):
            if far > 1:
                await_block(side, far, h, 0)

                @pl.when(gets(side, far))
                def _():
                    for at in range(0, tokens, tile):
                        weights, keep = masked(h, source(side, far), at)
                        wb[side, pl.ds(at, tile)] = weights
                        acc[h, pl.ds(at, tile)] = acc[h, pl.ds(at, tile)] * keep

        if far > 1:
            for side in (LEFT, RIGHT):
                await_block(side, far, h, 1)

        def finish(p):
            for at in range(0, rows, tile):
                cut = pl.ds(pl.multiple_of(p * rows + at, tile), tile)
                if far > 1:
                    for side in (LEFT, RIGHT):

                        @pl.when(gets(side, far))
                        def _():
                            acc[h, cut] = acc[h, cut] + mixed(
                                wb[side, cut], h, source(side, far)
                            )

                ob[h, cut] = (acc[h, cut] / total[h, cut]).astype(jnp.bfloat16)

        for j in range(1, parts):
            finish(peer(j))
            o_exchange(h, j).start()
        finish(part)
        o_keep(h).start()

    each_head(last)

    def close_head(h):
        o_keep(h).wait()
        for j in range(1, parts):
            o_exchange(h, j).wait()
            q_exchange(h, j).wait_send()
            kv_exchange(h, j, 0, k_ref).wait_send()
            kv_exchange(h, j, 1, v_ref).wait_send()

        @pl.loop(1, far + 1)
        def _(step):
            for side in (LEFT, RIGHT):

                @pl.when(can_send(side, step))
                def _():
                    for p in range(parts):
                        for i in (0, 1):
                            hop(side, step, h, p, i).wait_send()

    each_head(close_head)


def shards(frames, parts, queries, keys, values, flags, widths):
    shape = queries.shape
    columns, features = shape[2], shape[3]
    rows = shape[1] * columns
    heads = features // HEAD_DIM // parts
    tokens = rows * parts
    far = frames - 2
    flat = [a.reshape(rows, features) for a in (queries, keys, values)]
    any_spec = pl.BlockSpec(memory_space=pl.ANY)
    others = max(parts - 1, 1)
    dma = pltpu.SemaphoreType.DMA
    out = pl.pallas_call(
        functools.partial(kernel, frames, parts, heads, columns),
        out_shape=pltpu.VMEM((rows, features), jnp.bfloat16),
        in_specs=[any_spec] * 5,
        out_specs=pl.BlockSpec(memory_space=pltpu.VMEM),
        scratch_shapes=[
            pltpu.VMEM((frames, heads, 2, parts, rows, HEAD_DIM), jnp.bfloat16),
            pltpu.VMEM((heads, parts, rows, HEAD_DIM), jnp.bfloat16),
            pltpu.VMEM((heads, tokens, HEAD_DIM), jnp.bfloat16),
            pltpu.VMEM((tokens, tokens), jnp.float32),
            pltpu.VMEM((2, tokens, tokens), jnp.bfloat16),
            pltpu.VMEM((heads, tokens, 1), jnp.float32),
            pltpu.VMEM((heads, tokens, 1), jnp.float32),
            pltpu.VMEM((heads, tokens, HEAD_DIM), jnp.float32),
            dma((3, heads)),
            dma((2, others, heads)),
            dma((2, others, heads)),
            dma((others, heads)),
            dma((others, heads)),
            dma((2, far, heads, parts, 2)),
            dma((2, far, heads, parts, 2)),
            dma((heads,)),
            dma((others, heads)),
            dma((others, heads)),
            pltpu.SMEM(flags.shape, jnp.int32),
            pltpu.SMEM(widths.shape, jnp.int32),
            dma((2,)),
        ],
        compiler_params=pltpu.CompilerParams(collective_id=0, has_side_effects=True),
    )(*flat, flags, widths)
    return out.reshape(shape)


def solution(mesh):
    spec = P(("group", "frame"), "space", None, "head")
    return jax.shard_map(
        functools.partial(shards, mesh.shape["frame"], mesh.shape["space"]),
        mesh=mesh,
        in_specs=(spec, spec, spec, P(), P()),
        out_specs=spec,
        check_vma=False,
    )
```

```python
import functools
import math

import jax
import jax.numpy as jnp
from jax import lax
from jax.experimental import pallas as pl
from jax.experimental.pallas import tpu as pltpu
from jax.sharding import PartitionSpec as P

HEAD_DIM = 128
NEG_FILL = -1e30
SCALE = math.log2(math.e) / HEAD_DIM**0.5
MESH = pl.DeviceIdType.MESH


def kernel(
    frames,
    parts,
    heads,
    columns,
    q_ref,
    k_ref,
    v_ref,
    flags_in,
    widths_in,
    out_ref,
    kv,
    qb,
    ob,
    dist,
    wb,
    top,
    total,
    acc,
    local_sem,
    xkv_send,
    xkv_recv,
    xq_send,
    xq_recv,
    z_send,
    z_recv,
    o_local,
    o_send,
    o_recv,
    flags_ref,
    widths_ref,
    table_sem,
):
    frame = lax.axis_index("frame")
    part = lax.axis_index("space")
    rows = q_ref.shape[0]
    tokens = parts * rows
    tile = rows
    far = frames - 2
    LEFT, RIGHT = 0, 1

    def lanes(ref, head):
        return ref.at[:, pl.ds(pl.multiple_of(head * HEAD_DIM, HEAD_DIM), HEAD_DIM)]

    def peer(j):
        return lax.rem(part + j, parts)

    barrier = pltpu.get_barrier_semaphore()
    for j in range(1, parts):
        pl.semaphore_signal(barrier, inc=1, device_id={"space": peer(j)}, device_id_type=MESH)

    @pl.when(frame > 0)
    def _():
        pl.semaphore_signal(barrier, inc=1, device_id={"frame": frame - 1}, device_id_type=MESH)

    @pl.when(frame < frames - 1)
    def _():
        pl.semaphore_signal(barrier, inc=1, device_id={"frame": frame + 1}, device_id_type=MESH)

    def local_copies(h):
        mine = part * heads + h
        return (
            pltpu.make_async_copy(lanes(k_ref, mine), kv.at[frame, h, 0, part], local_sem.at[0, h]),
            pltpu.make_async_copy(lanes(v_ref, mine), kv.at[frame, h, 1, part], local_sem.at[1, h]),
            pltpu.make_async_copy(lanes(q_ref, mine), qb.at[h, part], local_sem.at[2, h]),
        )

    def kv_exchange(h, j, i, src_ref):
        return pltpu.make_async_remote_copy(
            src_ref=lanes(src_ref, peer(j) * heads + h),
            dst_ref=kv.at[frame, h, i, part],
            send_sem=xkv_send.at[i, j - 1, h],
            recv_sem=xkv_recv.at[i, j - 1, h],
            device_id={"space": peer(j)},
            device_id_type=MESH,
        )

    def q_exchange(h, j):
        return pltpu.make_async_remote_copy(
            src_ref=lanes(q_ref, peer(j) * heads + h),
            dst_ref=qb.at[h, part],
            send_sem=xq_send.at[j - 1, h],
            recv_sem=xq_recv.at[j - 1, h],
            device_id={"space": peer(j)},
            device_id_type=MESH,
        )

    def o_exchange(h, j):
        return pltpu.make_async_remote_copy(
            src_ref=ob.at[h, pl.ds(pl.multiple_of(peer(j) * rows, rows), rows)],
            dst_ref=lanes(out_ref, part * heads + h),
            send_sem=o_send.at[j - 1, h],
            recv_sem=o_recv.at[j - 1, h],
            device_id={"space": peer(j)},
            device_id_type=MESH,
        )

    def o_keep(h):
        return pltpu.make_async_copy(
            ob.at[h, pl.ds(pl.multiple_of(part * rows, rows), rows)],
            lanes(out_ref, part * heads + h),
            o_local.at[h],
        )

    def hop(side, step, h, p, i, src=None):
        towards = 1 if side == RIGHT else -1
        owner = frame - towards * (step - 1)
        return pltpu.make_async_remote_copy(
            src_ref=kv.at[owner, h, i, p] if src is None else src,
            dst_ref=kv.at[owner, h, i, p],
            send_sem=z_send.at[side, step - 1, h, p, i],
            recv_sem=z_recv.at[side, step - 1, h, p, i],
            device_id={"frame": frame + towards},
            device_id_type=MESH,
        )

    def can_send(side, step):
        if side == RIGHT:
            return (frame < frames - 1) & (frame - (step - 1) >= 0)
        return (frame > 0) & (frame + (step - 1) <= frames - 1)

    def gets(side, step):
        if side == RIGHT:
            return frame - step >= 0
        return frame + step <= frames - 1

    def landed(side, step, h, p, i):
        towards = 1 if side == RIGHT else -1
        owner = frame - towards * step
        return pltpu.make_async_remote_copy(
            src_ref=kv.at[owner, h, i, p],
            dst_ref=kv.at[owner, h, i, p],
            send_sem=z_send.at[side, step - 1, h, p, i],
            recv_sem=z_recv.at[side, step - 1, h, p, i],
            device_id={"frame": frame - towards},
            device_id_type=MESH,
        )

    def each_head(body):
        @pl.loop(0, heads)
        def _(h):
            body(h)

    pl.semaphore_wait(
        barrier,
        parts - 1 + jnp.where(frame > 0, 1, 0) + jnp.where(frame < frames - 1, 1, 0),
    )

    def open_head(h):
        mine = part * heads + h
        for j in range(1, parts):
            kv_exchange(h, j, 0, k_ref).start()
            kv_exchange(h, j, 1, v_ref).start()
        for side in (LEFT, RIGHT):

            @pl.when(can_send(side, 1))
            def _():
                hop(side, 1, h, part, 0, lanes(k_ref, mine)).start()
                hop(side, 1, h, part, 1, lanes(v_ref, mine)).start()

    each_head(open_head)

    tables = (
        pltpu.make_async_copy(flags_in, flags_ref, table_sem.at[0]),
        pltpu.make_async_copy(widths_in, widths_ref, table_sem.at[1]),
    )
    for copy in tables:
        copy.start()

    def open_queries(h):
        for copy in local_copies(h):
            copy.start()
        for j in range(1, parts):
            q_exchange(h, j).start()

    each_head(open_queries)

    def row_of(axis):
        at = lax.broadcasted_iota(jnp.int32, (tokens, tokens), axis).astype(jnp.float32)
        return jnp.floor((at + 0.5) * (1.0 / columns))

    dist[...] = jnp.abs(row_of(0) - row_of(1))
    top[...] = jnp.full(top.shape, NEG_FILL, jnp.float32)
    total[...] = jnp.zeros(total.shape, jnp.float32)
    acc[...] = jnp.zeros(acc.shape, jnp.float32)

    def pass_parts(h):
        for j in range(1, parts):
            p = lax.rem(part - j + parts, parts)
            for i in (0, 1):
                kv_exchange(h, j, i, (k_ref, v_ref)[i]).wait_recv()
            for side in (LEFT, RIGHT):

                @pl.when(can_send(side, 1))
                def _():
                    for i in (0, 1):
                        hop(side, 1, h, p, i).start()

    each_head(pass_parts)
    for copy in tables:
        copy.wait()

    def masked(h, g, at):
        gap = jnp.abs(frame - g)
        reach = jnp.where(flags_ref[frame, g] > 0, widths_ref[gap], -1).astype(jnp.float32)
        cut = pl.ds(at, tile)
        queries = qb[h].reshape(tokens, HEAD_DIM)[at : at + tile]
        keys = kv[g, h, 0].reshape(tokens, HEAD_DIM)
        scores = lax.dot_general(
            queries, keys, (((1,), (1,)), ((), ())), preferred_element_type=jnp.float32
        )
        scores = jnp.where(dist[cut, :] <= reach, scores, NEG_FILL)
        old_top = top[h, cut]
        new_top = jnp.maximum(old_top, jnp.max(scores, axis=1, keepdims=True))
        weights = jnp.exp2((scores - new_top) * SCALE)
        keep = jnp.exp2((old_top - new_top) * SCALE)
        top[h, cut] = new_top
        total[h, cut] = total[h, cut] * keep + jnp.sum(weights, axis=1, keepdims=True)
        return weights.astype(jnp.bfloat16), keep

    def mixed(weights, h, g):
        vals = kv[g, h, 1].reshape(tokens, HEAD_DIM)
        return jnp.dot(weights, vals, preferred_element_type=jnp.float32)

    def update(h, g):
        for at in range(0, tokens, tile):
            cut = pl.ds(at, tile)
            weights, keep = masked(h, g, at)
            acc[h, cut] = acc[h, cut] * keep + mixed(weights, h, g)

    def await_block(side, step, h, i):
        @pl.when(gets(side, step))
        def _():
            for p in range(parts):
                landed(side, step, h, p, i).wait_recv()

    def source(side, step):
        return frame - step if side == RIGHT else frame + step

    def near(step, h, relay):
        for side in (LEFT, RIGHT):
            for i in (0, 1):
                await_block(side, step, h, i)
            if relay:

                @pl.when(gets(side, step) & can_send(side, step + 1))
                def _():
                    for i in (0, 1):
                        for p in range(parts):
                            hop(side, step + 1, h, p, i).start()

    def blend(step, h):
        for side in (LEFT, RIGHT):

            @pl.when(gets(side, step))
            def _():
                update(h, source(side, step))

    def first(h):
        near(1, h, far > 1)
        for copy in local_copies(h):
            copy.wait()
        for j in range(1, parts):
            q_exchange(h, j).wait_recv()
        update(h, frame)
        blend(1, h)

    each_head(first)

    if far > 2:

        @pl.loop(2, far)
        def _(step):
            def middle(h):
                near(step, h, True)
                blend(step, h)

            each_head(middle)

    def last(h):
        for side in (LEFT, RIGHT):
            if far > 1:
                await_block(side, far, h, 0)

                @pl.when(gets(side, far))
                def _():
                    for at in range(0, tokens, tile):
                        weights, keep = masked(h, source(side, far), at)
                        wb[side, pl.ds(at, tile)] = weights
                        acc[h, pl.ds(at, tile)] = acc[h, pl.ds(at, tile)] * keep

        total[h] = 1.0 / total[h]
        if far > 1:
            for side in (LEFT, RIGHT):
                await_block(side, far, h, 1)

        def finish(p):
            for at in range(0, rows, tile):
                cut = pl.ds(pl.multiple_of(p * rows + at, tile), tile)
                if far > 1:
                    for side in (LEFT, RIGHT):

                        @pl.when(gets(side, far))
                        def _():
                            acc[h, cut] = acc[h, cut] + mixed(
                                wb[side, cut], h, source(side, far)
                            )

                ob[h, cut] = (acc[h, cut] * total[h, cut]).astype(jnp.bfloat16)

        for j in range(1, parts):
            finish(peer(j))
            o_exchange(h, j).start()
        finish(part)
        o_keep(h).start()

    each_head(last)

    def close_head(h):
        o_keep(h).wait()
        for j in range(1, parts):
            o_exchange(h, j).wait()
            q_exchange(h, j).wait_send()
            kv_exchange(h, j, 0, k_ref).wait_send()
            kv_exchange(h, j, 1, v_ref).wait_send()

        @pl.loop(1, far + 1)
        def _(step):
            for side in (LEFT, RIGHT):

                @pl.when(can_send(side, step))
                def _():
                    for p in range(parts):
                        for i in (0, 1):
                            hop(side, step, h, p, i).wait_send()

    each_head(close_head)


def shards(frames, parts, queries, keys, values, flags, widths):
    shape = queries.shape
    columns, features = shape[2], shape[3]
    rows = shape[1] * columns
    heads = features // HEAD_DIM // parts
    tokens = rows * parts
    far = frames - 2
    flat = [a.reshape(rows, features) for a in (queries, keys, values)]
    any_spec = pl.BlockSpec(memory_space=pl.ANY)
    others = max(parts - 1, 1)
    dma = pltpu.SemaphoreType.DMA
    out = pl.pallas_call(
        functools.partial(kernel, frames, parts, heads, columns),
        out_shape=pltpu.VMEM((rows, features), jnp.bfloat16),
        in_specs=[any_spec] * 5,
        out_specs=pl.BlockSpec(memory_space=pltpu.VMEM),
        scratch_shapes=[
            pltpu.VMEM((frames, heads, 2, parts, rows, HEAD_DIM), jnp.bfloat16),
            pltpu.VMEM((heads, parts, rows, HEAD_DIM), jnp.bfloat16),
            pltpu.VMEM((heads, tokens, HEAD_DIM), jnp.bfloat16),
            pltpu.VMEM((tokens, tokens), jnp.float32),
            pltpu.VMEM((2, tokens, tokens), jnp.bfloat16),
            pltpu.VMEM((heads, tokens, 1), jnp.float32),
            pltpu.VMEM((heads, tokens, 1), jnp.float32),
            pltpu.VMEM((heads, tokens, HEAD_DIM), jnp.float32),
            dma((3, heads)),
            dma((2, others, heads)),
            dma((2, others, heads)),
            dma((others, heads)),
            dma((others, heads)),
            dma((2, far, heads, parts, 2)),
            dma((2, far, heads, parts, 2)),
            dma((heads,)),
            dma((others, heads)),
            dma((others, heads)),
            pltpu.SMEM(flags.shape, jnp.int32),
            pltpu.SMEM(widths.shape, jnp.int32),
            dma((2,)),
        ],
        compiler_params=pltpu.CompilerParams(collective_id=0, has_side_effects=True),
    )(*flat, flags, widths)
    return out.reshape(shape)


def solution(mesh):
    spec = P(("group", "frame"), "space", None, "head")
    return jax.shard_map(
        functools.partial(shards, mesh.shape["frame"], mesh.shape["space"]),
        mesh=mesh,
        in_specs=(spec, spec, spec, P(), P()),
        out_specs=spec,
        check_vma=False,
    )
```
